32 devices in a mesh: seq: 16 (over z, y, x), head: 2 (over core).
Axes of the slice: x: 2, y: 2, z: 4, core: 2. Of those that a mesh axis runs over, the one named last changes fastest.
Arguments:
- query_tok: bfloat16 [6144, 1536], P('seq', 'head'), may hold values from -110 to 110
- key_tok: bfloat16 [6144, 1536], P('seq', 'head'), may hold values from -5 to 5
- value_tok: bfloat16 [6144, 1536], P('seq', 'head'), may hold values from -6 to 6
- out_weight: bfloat16 [3072, 1536], P(None, 'head'), may hold values from -0.15625 to 0.15625
- grad_out: bfloat16 [6144, 3072], P('seq', 'head'), may hold values from -6 to 6
- tile_pairs: int32 [16, 7], P('seq'), may hold values from -1 to 15, as said below
Outputs:
- mixed_out: bfloat16 [6144, 3072], P('seq', 'head')
- grad_query: bfloat16 [6144, 1536], P('seq', 'head')
- grad_key: bfloat16 [6144, 1536], P('seq', 'head')
- grad_value: bfloat16 [6144, 1536], P('seq', 'head')
The draws below stay inside these ranges and needn't reach their ends.
Inputs may be any that keep to these rules, and one draw needn't show every extreme that they name: `tile_pairs`: slot j of tile g holds g + o_j or -1, with offsets o = (0, 1, -1, 8, -8, 16, -16); slot 0 always holds g; the list is symmetric: b is in the list of g exactly when g is in the list of b.
All inputs are finite; a program needn't handle non-finite values.
Results may differ from the reference program's by a relative error of at most 0.025.
Values may be sent and summed in bfloat16 or wider, within the bound.
A program may use at most 192 MiB of HBM per device.

```python
import jax
import jax.numpy as jnp
from jax import lax

D = 3072
HEADS = 12
HD = 128
TILE = 384
SLOTS = 7
GW_T = 8
TILES = 16
GH_T = 2
FRAME = 16
TOKENS = 6144


def shared_fields(key):
    query_key = jax.random.fold_in(key, 101)
    key_key = jax.random.fold_in(key, 102)
    shape = (TOKENS, HEADS * HD)
    key_field = jnp.clip(jax.random.normal(key_key, shape, jnp.float32), -4.0, 4.0)
    query_field = jnp.clip(jax.random.normal(query_key, shape, jnp.float32), -4.0, 4.0)
    return (query_field, key_field)


def draw_query_tok(key, part):
    return shared_fields(key)[0].astype(jnp.bfloat16)


def draw_key_tok(key, part):
    return shared_fields(key)[1].astype(jnp.bfloat16)


def draw_tile_pairs(key, part):
    tile_ids = jnp.arange(TILES, dtype=jnp.int32)
    column = tile_ids % GW_T
    tile_row = tile_ids // GW_T % GH_T
    keep_bits = jax.random.randint(jax.random.fold_in(key, 201), (TILES, 3), 0, 4) < 3
    right_pair = keep_bits[:, 0] & (column < GW_T - 1)
    down_pair = keep_bits[:, 2] & (tile_row < GH_T - 1) & (tile_ids + GW_T < TILES)
    later_pair = keep_bits[:, 1] & (tile_ids + FRAME < TILES)
    left_pair = jnp.roll(right_pair, 1) & (column > 0)
    up_pair = jnp.roll(down_pair, GW_T) & (tile_row > 0) & (tile_ids >= GW_T)
    earlier_pair = jnp.roll(later_pair, FRAME) & (tile_ids >= FRAME)
    absent = jnp.full((TILES,), -1, jnp.int32)
    columns = [tile_ids, jnp.where(right_pair, tile_ids + 1, absent), jnp.where(left_pair, tile_ids - 1, absent), jnp.where(down_pair, tile_ids + GW_T, absent), jnp.where(up_pair, tile_ids - GW_T, absent), jnp.where(later_pair, tile_ids + FRAME, absent), jnp.where(earlier_pair, tile_ids - FRAME, absent)]
    return jnp.stack(columns, axis=1).astype(jnp.int32)


def level_of(stream_key, shape, split, smallest, high):
    level, own = 1.0, jax.random.fold_in(stream_key, 6)
    for position, shards_of in split:
        draws = jnp.exp(jax.random.uniform(jax.random.fold_in(own, position), (shards_of,), jnp.float32, smallest / len(split), high / len(split)))
        level = level * jnp.repeat(draws, shape[position] // shards_of).reshape([-1 if axis == position else 1 for axis in range(len(shape))])
    return level


def scatter_about(stream_key, shape, deviation, bound, shards=(), kind=jnp.bfloat16):
    level = level_of(stream_key, shape, shards, -0.22, 0.18) if shards else 1.0
    values = jax.random.normal(stream_key, shape, jnp.float32) * deviation * level
    return jnp.minimum(jnp.maximum(values, -bound), bound).astype(kind)


def setup_inputs(seed: int = 0) -> dict:
    key_of = jax.random.split(jax.random.key(seed), 7)
    query_tok = draw_query_tok(jax.random.fold_in(key_of[6], 71), 0)
    key_tok = draw_key_tok(jax.random.fold_in(key_of[6], 71), 0)
    value_tok = scatter_about(key_of[2], (TOKENS, HEADS * HD), 1.0, 6.0, ((0, 16), (1, 2)))
    out_weight = scatter_about(key_of[3], (D, HEADS * HD), (HEADS * HD) ** -0.5, 0.15625, ((1, 2),))
    grad_out = scatter_about(key_of[4], (TOKENS, D), 1.0, 6.0, ((0, 16), (1, 2)))
    tile_pairs = draw_tile_pairs(jax.random.fold_in(key_of[6], 71), 0)
    return {"query_tok": query_tok, "key_tok": key_tok, "value_tok": value_tok, "out_weight": out_weight, "grad_out": grad_out, "tile_pairs": tile_pairs}


MASKED = -1.0e30


def merge_terms(terms):
    others = terms[1:].astype(jnp.bfloat16).astype(jnp.float32)
    return terms[0] + jnp.sum(others, axis=0)


def reference(query_tok, key_tok, value_tok, out_weight, grad_out, tile_pairs):
    score_scale = HD ** -0.5
    query_tiles = query_tok.reshape(TILES, TILE, HEADS, HD)
    key_tiles = key_tok.reshape(TILES, TILE, HEADS, HD)
    value_tiles = value_tok.reshape(TILES, TILE, HEADS, HD)
    present = tile_pairs >= 0
    safe_index = jnp.maximum(tile_pairs, 0).astype(jnp.int32)
    tile_ids = jnp.arange(TILES, dtype=jnp.int32)

    def forward_tile(tile_id):
        picks = safe_index[tile_id]
        col_mask = jnp.repeat(present[tile_id], TILE)
        queries = query_tiles[tile_id].astype(jnp.float32)
        near_keys = key_tiles[picks].reshape(SLOTS * TILE, HEADS, HD).astype(jnp.float32)
        near_values = value_tiles[picks].reshape(SLOTS * TILE, HEADS, HD).astype(jnp.float32)
        scores = jnp.einsum("qhd,khd->hqk", queries, near_keys) * score_scale
        scores = jnp.where(col_mask[None, None, :], scores, MASKED)
        row_max = jnp.max(scores, axis=-1, keepdims=True)
        log_total = row_max[..., 0] + jnp.log(jnp.sum(jnp.exp(scores - row_max), axis=-1))
        weights = jnp.exp(scores - log_total[..., None]).astype(jnp.bfloat16)
        attended = jnp.einsum("hqk,khd->qhd", weights.astype(jnp.float32), near_values).astype(jnp.bfloat16)
        return attended, log_total

    attended, log_totals = lax.map(forward_tile, tile_ids)
    attended_flat = attended.reshape(TOKENS, HEADS * HD)
    mixed_out = jnp.dot(attended_flat, out_weight.T, preferred_element_type=jnp.float32).astype(jnp.bfloat16)
    grad_attended = jnp.dot(grad_out, out_weight, preferred_element_type=jnp.float32).astype(jnp.bfloat16)
    products = grad_attended.astype(jnp.float32) * attended_flat.astype(jnp.float32)
    row_delta = jnp.sum(products.reshape(TILES, TILE, HEADS, HD), axis=-1).transpose(0, 2, 1)
    grad_tiles = grad_attended.reshape(TILES, TILE, HEADS, HD)

    def query_grads(tile_id):
        picks = safe_index[tile_id]
        col_mask = jnp.repeat(present[tile_id], TILE)
        queries = query_tiles[tile_id].astype(jnp.float32)
        near_keys = key_tiles[picks].reshape(SLOTS * TILE, HEADS, HD).astype(jnp.float32)
        near_values = value_tiles[picks].reshape(SLOTS * TILE, HEADS, HD).astype(jnp.float32)
        scores = jnp.einsum("qhd,khd->hqk", queries, near_keys) * score_scale
        scores = jnp.where(col_mask[None, None, :], scores, MASKED)
        weights = jnp.exp(scores - log_totals[tile_id][..., None])
        own_grads = grad_tiles[tile_id].astype(jnp.float32)
        grad_probs = jnp.einsum("qhd,khd->hqk", own_grads, near_values)
        grad_scores = (weights * (grad_probs - row_delta[tile_id][..., None]) * score_scale).astype(jnp.bfloat16)
        return jnp.einsum("hqk,khd->qhd", grad_scores.astype(jnp.float32), near_keys).astype(jnp.bfloat16)

    def key_grads(tile_id):
        picks = safe_index[tile_id]
        row_mask = jnp.repeat(present[tile_id], TILE)
        near_queries = query_tiles[picks].reshape(SLOTS * TILE, HEADS, HD).astype(jnp.float32)
        near_grads = grad_tiles[picks].reshape(SLOTS * TILE, HEADS, HD).astype(jnp.float32)
        near_lse = log_totals[picks].transpose(1, 0, 2).reshape(HEADS, SLOTS * TILE)
        near_delta = row_delta[picks].transpose(1, 0, 2).reshape(HEADS, SLOTS * TILE)
        own_keys = key_tiles[tile_id].astype(jnp.float32)
        own_values = value_tiles[tile_id].astype(jnp.float32)
        scores = jnp.einsum("qhd,khd->hqk", near_queries, own_keys) * score_scale
        scores = jnp.where(row_mask[None, :, None], scores, MASKED)
        weights = jnp.exp(scores - near_lse[..., None])
        weights_low = weights.astype(jnp.bfloat16).astype(jnp.float32).reshape(HEADS, SLOTS, TILE, TILE)
        grads_slots = near_grads.reshape(SLOTS, TILE, HEADS, HD)
        queries_slots = near_queries.reshape(SLOTS, TILE, HEADS, HD)
        value_terms = jnp.einsum("hsqk,sqhd->skhd", weights_low, grads_slots)
        grad_probs = jnp.einsum("qhd,khd->hqk", near_grads, own_values)
        grad_scores = (weights * (grad_probs - near_delta[..., None]) * score_scale).astype(jnp.bfloat16)
        scores_slots = grad_scores.astype(jnp.float32).reshape(HEADS, SLOTS, TILE, TILE)
        key_terms = jnp.einsum("hsqk,sqhd->skhd", scores_slots, queries_slots)
        return merge_terms(key_terms).astype(jnp.bfloat16), merge_terms(value_terms).astype(jnp.bfloat16)

    grad_query = lax.map(query_grads, tile_ids).reshape(TOKENS, HEADS * HD)
    grad_key, grad_value = lax.map(key_grads, tile_ids)
    return (mixed_out, grad_query, grad_key.reshape(TOKENS, HEADS * HD), grad_value.reshape(TOKENS, HEADS * HD))
```

```python
import functools

import jax
import jax.numpy as jnp
from jax import lax
from jax.experimental import pallas as pl
from jax.experimental.pallas import tpu as pltpu
from jax.sharding import PartitionSpec as P

HD = 128
GW_T = 8
MASKED = -1e30
LOG2E = 1.4426950408889634
MESH = pl.DeviceIdType.MESH
F32 = jnp.float32
BF16 = jnp.bfloat16


def slot_groups(tile_count):
    frame_tiles = min(4, tile_count // 8) * GW_T
    offsets = (0, 1, -1, GW_T, -GW_T, frame_tiles, -frame_tiles)
    groups = []
    for column, offset in enumerate(offsets):
        if abs(offset) >= tile_count:
            continue
        for group in groups:
            if (group[0] - offset) % tile_count == 0:
                group[1] = True
                group[2].append(column)
                break
        else:
            groups.append([offset, False, [column]])
    return groups


def dot(a, b, da, db):
    return lax.dot_general(a, b, (((da,), (db,)), ((), ())), preferred_element_type=F32)


def kernel(
    groups, tile_count, scale,
    pairs, q_in, k_in, v_in, w_in, g_in,
    mixed, gq, gk, gv,
    kv, qb, wb, gown, goth, gacc, dob, att, probs, acc, tsend, trecv, msend, mrecv,
    load_sem, kv_send, kv_recv, t_send, t_recv, x_send, x_recv,
):
    g = lax.axis_index("seq")
    c = lax.axis_index("head")
    other = 1 - c
    heads = qb.shape[0]
    rows = qb.shape[1]
    half = gown.shape[1]
    slots = len(groups)

    def place(step, wraps):
        at = g + step
        if wraps:
            return lax.rem(at + tile_count, tile_count), None
        ok = jnp.logical_and(at >= 0, at < tile_count)
        return jnp.clip(at, 0, tile_count - 1), ok

    def when(ok, fn):
        if ok is None:
            fn()
        else:
            pl.when(ok)(fn)

    source = [place(o, w) for o, w, _ in groups]
    target = [place(-o, w) for o, w, _ in groups]
    swaps = [s for s, (_, w, _) in enumerate(groups) if w]
    swap = swaps[0] if swaps else None
    hands_on = [None] * slots
    middle = tile_count // 2
    if swap is not None:
        for s, (o, _, _) in enumerate(groups):
            if abs(o) != 1:
                continue
            ends, near = ((tile_count - 1, middle), (0, middle - 1))[o > 0]
            relay = g == ends
            hands_on[s] = relay
            to, ok = target[s]
            crossing = g == (2 * middle - 1) - near
            target[s] = (
                jnp.where(relay, near, to),
                jnp.logical_or(relay, jnp.logical_and(ok, jnp.logical_not(crossing))),
            )
            at, ok = source[s]
            source[s] = (jnp.where(g == near, ends, at), ok)
    direct = [
        ok if hand is None else jnp.logical_and(ok, jnp.logical_not(hand))
        for (_, ok), hand in zip(target, hands_on)
    ]
    relays = [s for s in range(slots) if hands_on[s] is not None]
    relaying = None
    for s in relays:
        relaying = hands_on[s] if relaying is None else jnp.logical_or(relaying, hands_on[s])
    order = [0] + ([swap] if swap is not None else [])
    order += [s for s in range(slots) if s not in order]
    ahead = min(2, heads)

    barrier = pltpu.get_barrier_semaphore()
    pl.semaphore_signal(barrier, inc=1, device_id=(g, other), device_id_type=MESH)
    peers = 1
    for to, ok in target[1:] + source[1:]:

        def greet(to=to):
            pl.semaphore_signal(barrier, inc=1, device_id=(to, c), device_id_type=MESH)

        when(ok, greet)
        peers = peers + (1 if ok is None else ok.astype(jnp.int32))

    loads = []

    def load(src, dst):
        copy = pltpu.make_async_copy(src, dst, load_sem.at[len(loads)])
        copy.start()
        loads.append(copy)
        return copy

    kv_loads = []
    for h in range(heads):
        cols = pl.ds(h * HD, HD)
        kv_loads.append(
            (load(k_in.at[:, cols], kv.at[h, 0, 0]), load(v_in.at[:, cols], kv.at[h, 0, 1]))
        )
    own_load = load(g_in, gown)
    w_load = load(w_in, wb)
    q_loads = [load(q_in.at[:, pl.ds(h * HD, HD)], qb.at[h]) for h in range(heads)]

    pl.semaphore_wait(barrier, peers)

    def partner_copy(src, dst, i):
        return pltpu.make_async_remote_copy(
            src_ref=src, dst_ref=dst, send_sem=x_send.at[i], recv_sem=x_recv.at[i],
            device_id=(g, other), device_id_type=MESH,
        )

    def kv_copy(s, h, held=0):
        return pltpu.make_async_remote_copy(
            src_ref=kv.at[h, held], dst_ref=kv.at[h, s],
            send_sem=kv_send.at[s - 1, h], recv_sem=kv_recv.at[s - 1, h],
            device_id=(target[s][0], c), device_id_type=MESH,
        )

    def term_copy(s, h):
        return pltpu.make_async_remote_copy(
            src_ref=tsend.at[s - 1, h], dst_ref=trecv.at[s - 1, h],
            send_sem=t_send.at[s - 1, h], recv_sem=t_recv.at[s - 1, h],
            device_id=(source[s][0], c), device_id_type=MESH,
        )

    for h in range(heads):
        for copy in kv_loads[h]:
            copy.wait()
        for s in reversed(range(1, slots)):
            ok = direct[s]
            if h >= ahead and s == swap and relays:
                ok = jnp.logical_not(relaying)
            when(ok, lambda s=s, h=h: kv_copy(s, h).start())
    own_load.wait()
    grad_copy = partner_copy(gown, goth, 0)
    grad_copy.start()

    for s in range(1, slots):
        if source[s][1] is not None:

            def clear(s=s):
                def body(h, carry):
                    kv[h, s] = jnp.zeros(kv.shape[2:], BF16)
                    return carry

                lax.fori_loop(0, heads, body, 0)

            pl.when(jnp.logical_not(source[s][1]))(clear)

    w_load.wait()
    mine = pl.multiple_of(c * half, half)
    theirs = pl.multiple_of(other * half, half)

    def grad_own(h, carry):
        cols = pl.ds(pl.multiple_of(h * HD, HD), HD)
        gacc[h] = dot(gown[...], wb[pl.ds(mine, half), cols], 1, 0)
        return carry

    lax.fori_loop(0, heads, grad_own, 0)
    grad_copy.wait()

    def grad_other(h, carry):
        cols = pl.ds(pl.multiple_of(h * HD, HD), HD)
        dob[h] = (gacc[h] + dot(goth[...], wb[pl.ds(theirs, half), cols], 1, 0)).astype(BF16)
        return carry

    lax.fori_loop(0, heads, grad_other, 0)
    for copy in q_loads:
        copy.wait()

    biases = []
    for _, _, columns in groups:
        there = pairs[0, columns[0]]
        for column in columns[1:]:
            there = jnp.maximum(there, pairs[0, column])
        biases.append(jnp.where(there >= 0, 0.0, MASKED).astype(F32))
    rate = scale * LOG2E
    lag = min(3, heads)

    def hand_back(r, h):
        term_copy(r, h).wait_recv()
        both = tsend[swap - 1, h].astype(F32) + trecv[r - 1, h].astype(F32)
        tsend[swap - 1, h] = both.astype(BF16)
        term_copy(swap, h).start()

    def head(h, carry):
        cols = pl.ds(pl.multiple_of(h * HD, HD), HD)
        q = qb[h]
        do = dob[h]
        top = None
        for s in order:
            if s:
                when(source[s][1], lambda s=s: kv_copy(s, h).wait_recv())
            if s and s == swap:
                for r in relays:
                    when(hands_on[r], lambda r=r: kv_copy(r, h, swap).start())
                if relays:
                    now = jnp.logical_and(relaying, h + ahead < heads)
                    when(now, lambda: kv_copy(swap, h + ahead).start())
            scores = dot(kv[h, s, 0], q, 1, 1)
            probs[s] = scores
            peak = jnp.max(scores, axis=0, keepdims=True) + biases[s]
            top = peak if top is None else jnp.maximum(top, peak)
        total = None
        for s in range(slots):
            e = jnp.exp2((probs[s] - top) * rate + biases[s])
            probs[s] = e
            part = jnp.sum(e, axis=0, keepdims=True)
            total = part if total is None else total + part
        inverse = 1.0 / total
        out_t = None
        for s in range(slots):
            p = probs[s] * inverse
            probs[s] = p
            low = p.astype(BF16)
            part = dot(kv[h, s, 1], low, 0, 0)
            out_t = part if out_t is None else out_t + part
            term = dot(low, do, 1, 0)
            if s:
                tsend[s - 1, h, 1] = term.astype(BF16)
            else:
                acc[h, 1] = term
        delta = jnp.sum(do.astype(F32).T * out_t, axis=0, keepdims=True)
        att[:, cols] = out_t.T.astype(BF16)
        gq_t = None
        for s in range(slots):
            gp = dot(kv[h, s, 1], do, 1, 1)
            gs = (probs[s] * (gp - delta)).astype(BF16)
            term = dot(gs, q, 1, 0) * scale
            if s:
                tsend[s - 1, h, 0] = term.astype(BF16)
            else:
                acc[h, 0] = term
            part = dot(kv[h, s, 0], gs, 0, 0)
            gq_t = part if gq_t is None else gq_t + part
        gq[:, cols] = (gq_t * scale).T.astype(BF16)
        for s in reversed(range(1, slots)):
            ok = source[s][1]
            if s == swap and relays:
                ok = jnp.logical_not(relaying)
            when(ok, lambda s=s: term_copy(s, h).start())
        for r in relays:
            now = jnp.logical_and(hands_on[r], h >= lag)
            when(now, lambda r=r: hand_back(r, h - lag))
        return carry

    lax.fori_loop(0, heads, head, 0)

    def hand_back_rest(r):
        def body(h, carry):
            hand_back(r, h)
            return carry

        lax.fori_loop(heads - lag, heads, body, 0)

    for r in relays:
        when(hands_on[r], lambda r=r: hand_back_rest(r))

    wide = 256 if half % 256 == 0 else HD

    def project_other(j, carry):
        at = pl.multiple_of(j * wide, wide)
        msend[:, pl.ds(at, wide)] = dot(
            att[...], wb[pl.ds(pl.multiple_of(theirs + at, wide), wide), :], 1, 1
        ).astype(BF16)
        return carry

    lax.fori_loop(0, half // wide, project_other, 0)
    mixed_copy = partner_copy(msend, mrecv, 1)
    mixed_copy.start()

    def project_own(j, carry):
        at = pl.multiple_of(j * wide, wide)
        part = dot(att[...], wb[pl.ds(pl.multiple_of(mine + at, wide), wide), :], 1, 1)

        @pl.when(j == 0)
        def _():
            mixed_copy.wait_recv()

        mixed[:, pl.ds(at, wide)] = (part + mrecv[:, pl.ds(at, wide)].astype(F32)).astype(BF16)
        return carry

    lax.fori_loop(0, half // wide, project_own, 0)

    def finish(h, carry):
        cols = pl.ds(pl.multiple_of(h * HD, HD), HD)
        for s in reversed(range(1, slots)):

            def add(s=s):
                term_copy(s, h).wait_recv()
                acc[h] = acc[h] + trecv[s - 1, h].astype(F32)

            when(direct[s], add)
        gk[:, cols] = acc[h, 0].astype(BF16)
        gv[:, cols] = acc[h, 1].astype(BF16)
        return carry

    lax.fori_loop(0, heads, finish, 0)

    mixed_copy.wait_send()

    def drain(h, carry):
        for s in range(1, slots):
            when(target[s][1], lambda s=s: kv_copy(s, h).wait_send())
            when(source[s][1], lambda s=s: term_copy(s, h).wait_send())
        return carry

    lax.fori_loop(0, heads, drain, 0)


def on_device(query_tok, key_tok, value_tok, out_weight, grad_out, tile_pairs):
    rows, width = query_tok.shape
    heads = width // HD
    half = grad_out.shape[1]
    tile_count = lax.axis_size("seq")
    groups = slot_groups(tile_count)
    slots = len(groups)
    anywhere = pl.BlockSpec(memory_space=pl.ANY)
    in_vmem = pl.BlockSpec(memory_space=pltpu.VMEM)
    dma = pltpu.SemaphoreType.DMA
    near = (slots - 1, heads)
    return pl.pallas_call(
        functools.partial(kernel, groups, tile_count, HD ** (-0.5)),
        out_shape=(
            pltpu.VMEM((rows, half), BF16),
            pltpu.VMEM((rows, width), BF16),
            pltpu.VMEM((rows, width), BF16),
            pltpu.VMEM((rows, width), BF16),
        ),
        in_specs=[pl.BlockSpec(memory_space=pltpu.SMEM)] + [anywhere] * 5,
        out_specs=(in_vmem,) * 4,
        scratch_shapes=[
            pltpu.VMEM((heads, slots, 2, rows, HD), BF16),
            pltpu.VMEM((heads, rows, HD), BF16),
            pltpu.VMEM(out_weight.shape, BF16),
            pltpu.VMEM((rows, half), BF16),
            pltpu.VMEM((rows, half), BF16),
            pltpu.VMEM((heads, rows, HD), F32),
            pltpu.VMEM((heads, rows, HD), BF16),
            pltpu.VMEM((rows, width), BF16),
            pltpu.VMEM((slots, rows, rows), F32),
            pltpu.VMEM((heads, 2, rows, HD), F32),
            pltpu.VMEM(near + (2, rows, HD), BF16),
            pltpu.VMEM(near + (2, rows, HD), BF16),
            pltpu.VMEM((rows, half), BF16),
            pltpu.VMEM((rows, half), BF16),
            dma((3 * heads + 2,)),
            dma(near),
            dma(near),
            dma(near),
            dma(near),
            dma((2,)),
            dma((2,)),
        ],
        compiler_params=pltpu.CompilerParams(
            collective_id=0, has_side_effects=True, vmem_limit_bytes=52 * 2**20
        ),
        name="tile_attention",
    )(tile_pairs, query_tok, key_tok, value_tok, out_weight, grad_out)


def solution(mesh):
    in_specs = (
        P("seq", "head"),
        P("seq", "head"),
        P("seq", "head"),
        P(None, "head"),
        P("seq", "head"),
        P("seq", None),
    )
    out_specs = (P("seq", "head"), P("seq", "head"), P("seq", "head"), P("seq", "head"))
    return jax.shard_map(
        on_device, mesh=mesh, in_specs=in_specs, out_specs=out_specs, check_vma=False
    )
```

```python
import functools

import jax
import jax.numpy as jnp
from jax import lax
from jax.experimental import pallas as pl
from jax.experimental.pallas import tpu as pltpu
from jax.sharding import PartitionSpec as P

HD = 128
GW_T = 8
MASKED = -1e30
LOG2E = 1.4426950408889634
MESH = pl.DeviceIdType.MESH
F32 = jnp.float32
BF16 = jnp.bfloat16


def slot_groups(tile_count):
    frame_tiles = min(4, tile_count // 8) * GW_T
    offsets = (0, 1, -1, GW_T, -GW_T, frame_tiles, -frame_tiles)
    groups = []
    for column, offset in enumerate(offsets):
        if abs(offset) >= tile_count:
            continue
        for group in groups:
            if (group[0] - offset) % tile_count == 0:
                group[1] = True
                group[2].append(column)
                break
        else:
            groups.append([offset, False, [column]])
    return groups


def dot(a, b, da, db):
    return lax.dot_general(a, b, (((da,), (db,)), ((), ())), preferred_element_type=F32)


def kernel(
    groups, tile_count, scale,
    pairs_in, q_in, k_in, v_in, w_in, g_in,
    mixed, gq, gk, gv,
    pairs, kv, qb, wb, gown, goth, gacc, dob, att, probs, acc, tsend, trecv, msend, mrecv,
    load_sem, kv_send, kv_recv, t_send, t_recv, x_send, x_recv,
):
    g = lax.axis_index("seq")
    c = lax.axis_index("head")
    other = 1 - c
    heads = qb.shape[0]
    rows = qb.shape[1]
    half = gown.shape[1]
    slots = len(groups)

    def place(step, wraps):
        at = g + step
        if wraps:
            return lax.rem(at + tile_count, tile_count), None
        ok = jnp.logical_and(at >= 0, at < tile_count)
        return jnp.clip(at, 0, tile_count - 1), ok

    def when(ok, fn):
        if ok is None:
            fn()
        else:
            pl.when(ok)(fn)

    source = [place(o, w) for o, w, _ in groups]
    target = [place(-o, w) for o, w, _ in groups]
    swaps = [s for s, (_, w, _) in enumerate(groups) if w]
    swap = swaps[0] if swaps else None
    hands_on = [None] * slots
    middle = tile_count // 2
    if swap is not None:
        for s, (o, _, _) in enumerate(groups):
            if abs(o) != 1:
                continue
            ends, near = ((tile_count - 1, middle), (0, middle - 1))[o > 0]
            relay = g == ends
            hands_on[s] = relay
            to, ok = target[s]
            crossing = g == (2 * middle - 1) - near
            target[s] = (
                jnp.where(relay, near, to),
                jnp.logical_or(relay, jnp.logical_and(ok, jnp.logical_not(crossing))),
            )
            at, ok = source[s]
            source[s] = (jnp.where(g == near, ends, at), ok)
    direct = [
        ok if hand is None else jnp.logical_and(ok, jnp.logical_not(hand))
        for (_, ok), hand in zip(target, hands_on)
    ]
    relays = [s for s in range(slots) if hands_on[s] is not None]
    relaying = None
    for s in relays:
        relaying = hands_on[s] if relaying is None else jnp.logical_or(relaying, hands_on[s])
    order = [0] + ([swap] if swap is not None else [])
    order += [s for s in range(slots) if s not in order]
    ahead = min(2, heads)

    barrier = pltpu.get_barrier_semaphore()
    pl.semaphore_signal(barrier, inc=1, device_id=(g, other), device_id_type=MESH)
    peers = 1
    for to, ok in target[1:] + source[1:]:

        def greet(to=to):
            pl.semaphore_signal(barrier, inc=1, device_id=(to, c), device_id_type=MESH)

        when(ok, greet)
        peers = peers + (1 if ok is None else ok.astype(jnp.int32))

    loads = []

    def load(src, dst):
        copy = pltpu.make_async_copy(src, dst, load_sem.at[len(loads)])
        copy.start()
        loads.append(copy)
        return copy

    kv_loads = []
    for h in range(heads):
        cols = pl.ds(h * HD, HD)
        kv_loads.append(
            (load(k_in.at[:, cols], kv.at[h, 0, 0]), load(v_in.at[:, cols], kv.at[h, 0, 1]))
        )
    own_load = load(g_in, gown)
    pairs_load = load(pairs_in, pairs)
    w_load = load(w_in, wb)
    q_loads = [load(q_in.at[:, pl.ds(h * HD, HD)], qb.at[h]) for h in range(heads)]

    pl.semaphore_wait(barrier, peers)

    def partner_copy(src, dst, i):
        return pltpu.make_async_remote_copy(
            src_ref=src, dst_ref=dst, send_sem=x_send.at[i], recv_sem=x_recv.at[i],
            device_id=(g, other), device_id_type=MESH,
        )

    def kv_copy(s, h, held=0):
        return pltpu.make_async_remote_copy(
            src_ref=kv.at[h, held], dst_ref=kv.at[h, s],
            send_sem=kv_send.at[s - 1, h], recv_sem=kv_recv.at[s - 1, h],
            device_id=(target[s][0], c), device_id_type=MESH,
        )

    def term_copy(s, h):
        return pltpu.make_async_remote_copy(
            src_ref=tsend.at[s - 1, h], dst_ref=trecv.at[s - 1, h],
            send_sem=t_send.at[s - 1, h], recv_sem=t_recv.at[s - 1, h],
            device_id=(source[s][0], c), device_id_type=MESH,
        )

    for h in range(heads):
        for copy in kv_loads[h]:
            copy.wait()
        for s in reversed(range(1, slots)):
            ok = direct[s]
            if h >= ahead and s == swap and relays:
                ok = jnp.logical_not(relaying)
            when(ok, lambda s=s, h=h: kv_copy(s, h).start())
    own_load.wait()
    grad_copy = partner_copy(gown, goth, 0)
    grad_copy.start()

    for s in range(1, slots):
        if source[s][1] is not None:

            def clear(s=s):
                def body(h, carry):
                    kv[h, s] = jnp.zeros(kv.shape[2:], BF16)
                    return carry

                lax.fori_loop(0, heads, body, 0)

            pl.when(jnp.logical_not(source[s][1]))(clear)

    w_load.wait()
    mine = pl.multiple_of(c * half, half)
    theirs = pl.multiple_of(other * half, half)

    def grad_own(h, carry):
        cols = pl.ds(pl.multiple_of(h * HD, HD), HD)
        gacc[h] = dot(gown[...], wb[pl.ds(mine, half), cols], 1, 0)
        return carry

    lax.fori_loop(0, heads, grad_own, 0)
    grad_copy.wait()

    def grad_other(h, carry):
        cols = pl.ds(pl.multiple_of(h * HD, HD), HD)
        dob[h] = (gacc[h] + dot(goth[...], wb[pl.ds(theirs, half), cols], 1, 0)).astype(BF16)
        return carry

    lax.fori_loop(0, heads, grad_other, 0)
    for copy in q_loads:
        copy.wait()

    pairs_load.wait()
    biases = []
    for _, _, columns in groups:
        there = pairs[0, columns[0]]
        for column in columns[1:]:
            there = jnp.maximum(there, pairs[0, column])
        biases.append(jnp.where(there >= 0, 0.0, MASKED).astype(F32))
    rate = scale * LOG2E
    lag = min(3, heads)
    hold = min(2, heads)
    late = 2 * lax.rem(g, middle) >= middle
    holding = jnp.logical_and(late, jnp.logical_not(relaying)) if relays else late

    def hand_back(r, h):
        term_copy(r, h).wait_recv()
        both = tsend[swap - 1, h].astype(F32) + trecv[r - 1, h].astype(F32)
        tsend[swap - 1, h] = both.astype(BF16)
        term_copy(swap, h).start()

    def head(h, carry):
        cols = pl.ds(pl.multiple_of(h * HD, HD), HD)
        q = qb[h]
        do = dob[h]
        top = None
        for s in order:
            if s:
                when(source[s][1], lambda s=s: kv_copy(s, h).wait_recv())
            if s and s == swap:
                for r in relays:
                    when(hands_on[r], lambda r=r: kv_copy(r, h, swap).start())
                if relays:
                    now = jnp.logical_and(relaying, h + ahead < heads)
                    when(now, lambda: kv_copy(swap, h + ahead).start())
            scores = dot(kv[h, s, 0], q, 1, 1)
            probs[s] = scores
            peak = jnp.max(scores, axis=0, keepdims=True) + biases[s]
            top = peak if top is None else jnp.maximum(top, peak)
        total = None
        for s in range(slots):
            e = jnp.exp2((probs[s] - top) * rate + biases[s])
            probs[s] = e
            part = jnp.sum(e, axis=0, keepdims=True)
            total = part if total is None else total + part
        inverse = 1.0 / total
        out_t = None
        for s in range(slots):
            p = probs[s] * inverse
            probs[s] = p
            low = p.astype(BF16)
            part = dot(kv[h, s, 1], low, 0, 0)
            out_t = part if out_t is None else out_t + part
            term = dot(low, do, 1, 0)
            if s:
                tsend[s - 1, h, 1] = term.astype(BF16)
            else:
                acc[h, 1] = term
        delta = jnp.sum(do.astype(F32).T * out_t, axis=0, keepdims=True)
        att[:, cols] = out_t.T.astype(BF16)
        gq_t = None
        for s in range(slots):
            gp = dot(kv[h, s, 1], do, 1, 1)
            gs = (probs[s] * (gp - delta)).astype(BF16)
            term = dot(gs, q, 1, 0) * scale
            if s:
                tsend[s - 1, h, 0] = term.astype(BF16)
            else:
                acc[h, 0] = term
            part = dot(kv[h, s, 0], gs, 0, 0)
            gq_t = part if gq_t is None else gq_t + part
        gq[:, cols] = (gq_t * scale).T.astype(BF16)
        for s in reversed(range(1, slots)):
            ok = source[s][1]
            if s == swap:
                ok = jnp.logical_not(late)
                if relays:
                    ok = jnp.logical_and(ok, jnp.logical_not(relaying))
            when(ok, lambda s=s: term_copy(s, h).start())
        if swap is not None:
            now = jnp.logical_and(holding, h >= hold)
            when(now, lambda: term_copy(swap, h - hold).start())
        for r in relays:
            now = jnp.logical_and(hands_on[r], h >= lag)
            when(now, lambda r=r: hand_back(r, h - lag))
        return carry

    lax.fori_loop(0, heads, head, 0)

    def send_rest():
        def body(h, carry):
            term_copy(swap, h).start()
            return carry

        lax.fori_loop(heads - hold, heads, body, 0)

    if swap is not None:
        when(holding, send_rest)

    def hand_back_rest(r):
        def body(h, carry):
            hand_back(r, h)
            return carry

        lax.fori_loop(heads - lag, heads, body, 0)

    for r in relays:
        when(hands_on[r], lambda r=r: hand_back_rest(r))

    wide = 256 if half % 256 == 0 else HD

    def project_other(j, carry):
        at = pl.multiple_of(j * wide, wide)
        msend[:, pl.ds(at, wide)] = dot(
            att[...], wb[pl.ds(pl.multiple_of(theirs + at, wide), wide), :], 1, 1
        ).astype(BF16)
        return carry

    lax.fori_loop(0, half // wide, project_other, 0)
    mixed_copy = partner_copy(msend, mrecv, 1)
    mixed_copy.start()

    def project_own(j, carry):
        at = pl.multiple_of(j * wide, wide)
        part = dot(att[...], wb[pl.ds(pl.multiple_of(mine + at, wide), wide), :], 1, 1)

        @pl.when(j == 0)
        def _():
            mixed_copy.wait_recv()

        mixed[:, pl.ds(at, wide)] = (part + mrecv[:, pl.ds(at, wide)].astype(F32)).astype(BF16)
        return carry

    lax.fori_loop(0, half // wide, project_own, 0)

    def finish(h, carry):
        cols = pl.ds(pl.multiple_of(h * HD, HD), HD)
        for s in reversed(range(1, slots)):

            def add(s=s):
                term_copy(s, h).wait_recv()
                acc[h] = acc[h] + trecv[s - 1, h].astype(F32)

            when(direct[s], add)
        gk[:, cols] = acc[h, 0].astype(BF16)
        gv[:, cols] = acc[h, 1].astype(BF16)
        return carry

    lax.fori_loop(0, heads, finish, 0)

    mixed_copy.wait_send()

    def drain(h, carry):
        for s in range(1, slots):
            when(target[s][1], lambda s=s: kv_copy(s, h).wait_send())
            when(source[s][1], lambda s=s: term_copy(s, h).wait_send())
        return carry

    lax.fori_loop(0, heads, drain, 0)


def write_out(*refs):
    sems = refs[-1]
    copies = [
        pltpu.make_async_copy(src, dst, sems.at[i])
        for i, (src, dst) in enumerate(zip(refs[:4], refs[4:8]))
    ]
    for copy in copies:
        copy.start()
    for copy in copies:
        copy.wait()


def on_device(query_tok, key_tok, value_tok, out_weight, grad_out, tile_pairs):
    rows, width = query_tok.shape
    heads = width // HD
    half = grad_out.shape[1]
    tile_count = lax.axis_size("seq")
    groups = slot_groups(tile_count)
    slots = len(groups)
    anywhere = pl.BlockSpec(memory_space=pl.ANY)
    in_vmem = pl.BlockSpec(memory_space=pltpu.VMEM)
    dma = pltpu.SemaphoreType.DMA
    near = (slots - 1, heads)
    held = pl.pallas_call(
        functools.partial(kernel, groups, tile_count, HD ** (-0.5)),
        out_shape=(
            pltpu.VMEM((rows, half), BF16),
            pltpu.VMEM((rows, width), BF16),
            pltpu.VMEM((rows, width), BF16),
            pltpu.VMEM((rows, width), BF16),
        ),
        in_specs=[anywhere] * 6,
        out_specs=(in_vmem,) * 4,
        scratch_shapes=[
            pltpu.SMEM(tile_pairs.shape, jnp.int32),
            pltpu.VMEM((heads, slots, 2, rows, HD), BF16),
            pltpu.VMEM((heads, rows, HD), BF16),
            pltpu.VMEM(out_weight.shape, BF16),
            pltpu.VMEM((rows, half), BF16),
            pltpu.VMEM((rows, half), BF16),
            pltpu.VMEM((heads, rows, HD), F32),
            pltpu.VMEM((heads, rows, HD), BF16),
            pltpu.VMEM((rows, width), BF16),
            pltpu.VMEM((slots, rows, rows), F32),
            pltpu.VMEM((heads, 2, rows, HD), F32),
            pltpu.VMEM(near + (2, rows, HD), BF16),
            pltpu.VMEM(near + (2, rows, HD), BF16),
            pltpu.VMEM((rows, half), BF16),
            pltpu.VMEM((rows, half), BF16),
            dma((3 * heads + 3,)),
            dma(near),
            dma(near),
            dma(near),
            dma(near),
            dma((2,)),
            dma((2,)),
        ],
        compiler_params=pltpu.CompilerParams(
            collective_id=0, has_side_effects=True, vmem_limit_bytes=52 * 2**20
        ),
        name="tile_attention",
    )(tile_pairs, query_tok, key_tok, value_tok, out_weight, grad_out)
    return pl.pallas_call(
        write_out,
        out_shape=tuple(jax.ShapeDtypeStruct(x.shape, x.dtype) for x in held),
        in_specs=[in_vmem] * 4,
        out_specs=(anywhere,) * 4,
        scratch_shapes=[dma((4,))],
        name="write_out",
    )(*[pltpu.with_memory_space_constraint(x, pltpu.VMEM) for x in held])


def solution(mesh):
    in_specs = (
        P("seq", "head"),
        P("seq", "head"),
        P("seq", "head"),
        P(None, "head"),
        P("seq", "head"),
        P("seq", None),
    )
    out_specs = (P("seq", "head"), P("seq", "head"), P("seq", "head"), P("seq", "head"))
    return jax.shard_map(
        on_device, mesh=mesh, in_specs=in_specs, out_specs=out_specs, check_vma=False
    )
```

```python
import functools

import jax
import jax.numpy as jnp
from jax import lax
from jax.experimental import pallas as pl
from jax.experimental.pallas import tpu as pltpu
from jax.sharding import PartitionSpec as P

HD = 128
GW_T = 8
MASKED = -1e30
LOG2E = 1.4426950408889634
MESH = pl.DeviceIdType.MESH
F32 = jnp.float32
BF16 = jnp.bfloat16


def slot_groups(tile_count):
    frame_tiles = min(4, tile_count // 8) * GW_T
    offsets = (0, 1, -1, GW_T, -GW_T, frame_tiles, -frame_tiles)
    groups = []
    for column, offset in enumerate(offsets):
        if abs(offset) >= tile_count:
            continue
        for group in groups:
            if (group[0] - offset) % tile_count == 0:
                group[1] = True
                group[2].append(column)
                break
        else:
            groups.append([offset, False, [column]])
    return groups


def dot(a, b, da, db):
    return lax.dot_general(a, b, (((da,), (db,)), ((), ())), preferred_element_type=F32)


def kernel(
    groups, tile_count, scale,
    pairs_in, q_in, k_in, v_in, w_in, g_in,
    mixed, gq, gk, gv,
    pairs, kv, qb, wb, gown, goth, gacc, dob, att, probs, acc, tsend, trecv, msend, mrecv,
    ready, load_sem, kv_send, kv_recv, t_send, t_recv, x_send, x_recv,
):
    g = lax.axis_index("seq")
    c = lax.axis_index("head")
    other = 1 - c
    heads = qb.shape[0]
    rows = qb.shape[1]
    half = gown.shape[1]
    slots = len(groups)

    def place(step, wraps):
        at = g + step
        if wraps:
            return lax.rem(at + tile_count, tile_count), None
        ok = jnp.logical_and(at >= 0, at < tile_count)
        return jnp.clip(at, 0, tile_count - 1), ok

    def when(ok, fn):
        if ok is None:
            fn()
        else:
            pl.when(ok)(fn)

    source = [place(o, w) for o, w, _ in groups]
    target = [place(-o, w) for o, w, _ in groups]
    swaps = [s for s, (_, w, _) in enumerate(groups) if w]
    swap = swaps[0] if swaps else None
    hands_on = [None] * slots
    middle = tile_count // 2
    if swap is not None:
        for s, (o, _, _) in enumerate(groups):
            if abs(o) != 1:
                continue
            ends, near = ((tile_count - 1, middle), (0, middle - 1))[o > 0]
            relay = g == ends
            hands_on[s] = relay
            to, ok = target[s]
            crossing = g == (2 * middle - 1) - near
            target[s] = (
                jnp.where(relay, near, to),
                jnp.logical_or(relay, jnp.logical_and(ok, jnp.logical_not(crossing))),
            )
            at, ok = source[s]
            source[s] = (jnp.where(g == near, ends, at), ok)
    direct = [
        ok if hand is None else jnp.logical_and(ok, jnp.logical_not(hand))
        for (_, ok), hand in zip(target, hands_on)
    ]
    relays = [s for s in range(slots) if hands_on[s] is not None]
    relaying = None
    for s in relays:
        relaying = hands_on[s] if relaying is None else jnp.logical_or(relaying, hands_on[s])
    order = [0] + ([swap] if swap is not None else [])
    order += [s for s in range(slots) if s not in order]
    ahead = min(2, heads)

    barrier = pltpu.get_barrier_semaphore()
    pl.semaphore_signal(barrier, inc=1, device_id=(g, other), device_id_type=MESH)
    peers = 1
    answers = [(0, middle - 1), (middle, tile_count - 1)]
    if middle >= 4:
        answers.append((middle + middle // 2, middle + middle // 2 - 1))
    if not relays:
        answers = []
    for to, ok in target[1:] + [source[s] for s in range(1, slots) if s != swap]:
        greets, counts = ok, ok
        for early, late in answers:
            greets = jnp.logical_and(greets, jnp.logical_not((g == late) & (to == early))) if ok is not None else None
            counts = jnp.logical_and(counts, jnp.logical_not((g == early) & (to == late))) if ok is not None else None

        def greet(to=to):
            pl.semaphore_signal(barrier, inc=1, device_id=(to, c), device_id_type=MESH)

        when(greets, greet)
        peers = peers + (1 if counts is None else counts.astype(jnp.int32))

    loads = []

    def load(src, dst):
        copy = pltpu.make_async_copy(src, dst, load_sem.at[len(loads)])
        copy.start()
        loads.append(copy)
        return copy

    kv_loads = []
    for h in range(heads):
        cols = pl.ds(h * HD, HD)
        kv_loads.append(
            (load(k_in.at[:, cols], kv.at[h, 0, 0]), load(v_in.at[:, cols], kv.at[h, 0, 1]))
        )
    own_load = load(g_in, gown)
    pairs_load = load(pairs_in, pairs)
    w_load = load(w_in, wb)
    q_loads = [load(q_in.at[:, pl.ds(h * HD, HD)], qb.at[h]) for h in range(heads)]

    pl.semaphore_wait(barrier, peers)
    for early, late in answers:

        def answer(early=early):
            pl.semaphore_signal(ready, inc=1, device_id=(early, c), device_id_type=MESH)

        pl.when(g == late)(answer)

    def hear():
        pl.semaphore_wait(ready, 1)

    def partner_copy(src, dst, i):
        return pltpu.make_async_remote_copy(
            src_ref=src, dst_ref=dst, send_sem=x_send.at[i], recv_sem=x_recv.at[i],
            device_id=(g, other), device_id_type=MESH,
        )

    def kv_copy(s, h, held=0):
        return pltpu.make_async_remote_copy(
            src_ref=kv.at[h, held], dst_ref=kv.at[h, s],
            send_sem=kv_send.at[s - 1, h], recv_sem=kv_recv.at[s - 1, h],
            device_id=(target[s][0], c), device_id_type=MESH,
        )

    def term_copy(s, h):
        return pltpu.make_async_remote_copy(
            src_ref=tsend.at[s - 1, h], dst_ref=trecv.at[s - 1, h],
            send_sem=t_send.at[s - 1, h], recv_sem=t_recv.at[s - 1, h],
            device_id=(source[s][0], c), device_id_type=MESH,
        )

    def send_swap_tile(h, side=None):
        if swap is None or h >= heads:
            return
        ok = side
        if h >= ahead and relays:
            ok = jnp.logical_not(relaying)
            ok = ok if side is None else jnp.logical_and(side, ok)
        when(ok, lambda: kv_copy(swap, h).start())

    for copy in kv_loads[0]:
        copy.wait()
    send_swap_tile(0)
    if len(answers) > 2:
        pl.when(g == answers[2][0])(hear)
    for h in range(heads):
        if h + 1 < heads:
            for copy in kv_loads[h + 1]:
                copy.wait()
        send_swap_tile(h + 1, c == 0)
        for s in reversed(range(1, slots)):
            if s != swap:
                when(direct[s], lambda s=s, h=h: kv_copy(s, h).start())
        send_swap_tile(h + 1, c != 0)
    own_load.wait()
    grad_copy = partner_copy(gown, goth, 0)
    grad_copy.start()

    for s in range(1, slots):
        if source[s][1] is not None:

            def clear(s=s):
                def body(h, carry):
                    kv[h, s] = jnp.zeros(kv.shape[2:], BF16)
                    return carry

                lax.fori_loop(0, heads, body, 0)

            pl.when(jnp.logical_not(source[s][1]))(clear)

    w_load.wait()
    mine = pl.multiple_of(c * half, half)
    theirs = pl.multiple_of(other * half, half)

    def grad_own(h, carry):
        cols = pl.ds(pl.multiple_of(h * HD, HD), HD)
        gacc[h] = dot(gown[...], wb[pl.ds(mine, half), cols], 1, 0)
        return carry

    lax.fori_loop(0, heads, grad_own, 0)
    grad_copy.wait()

    def grad_other(h, carry):
        cols = pl.ds(pl.multiple_of(h * HD, HD), HD)
        dob[h] = (gacc[h] + dot(goth[...], wb[pl.ds(theirs, half), cols], 1, 0)).astype(BF16)
        return carry

    lax.fori_loop(0, heads, grad_other, 0)
    if answers:
        pl.when(jnp.logical_or(g == answers[0][0], g == answers[1][0]))(hear)
    for copy in q_loads:
        copy.wait()

    pairs_load.wait()
    biases = []
    for _, _, columns in groups:
        there = pairs[0, columns[0]]
        for column in columns[1:]:
            there = jnp.maximum(there, pairs[0, column])
        biases.append(jnp.where(there >= 0, 0.0, MASKED).astype(F32))
    rate = scale * LOG2E
    lag = min(3, heads)
    hold = min(1, heads)
    late = 2 * lax.rem(g, middle) >= middle
    holding = jnp.logical_and(late, jnp.logical_not(relaying)) if relays else late

    def hand_back(r, h):
        term_copy(r, h).wait_recv()
        both = tsend[swap - 1, h].astype(F32) + trecv[r - 1, h].astype(F32)
        tsend[swap - 1, h] = both.astype(BF16)
        term_copy(swap, h).start()

    def head(h, carry):
        cols = pl.ds(pl.multiple_of(h * HD, HD), HD)
        q = qb[h]
        do = dob[h]
        top = None
        for s in order:
            if s:
                when(source[s][1], lambda s=s: kv_copy(s, h).wait_recv())
            if s and s == swap:
                for r in relays:
                    when(hands_on[r], lambda r=r: kv_copy(r, h, swap).start())
                if relays:
                    now = jnp.logical_and(relaying, h + ahead < heads)
                    when(now, lambda: kv_copy(swap, h + ahead).start())
            scores = dot(kv[h, s, 0], q, 1, 1)
            probs[s] = scores
            peak = jnp.max(scores, axis=0, keepdims=True) + biases[s]
            top = peak if top is None else jnp.maximum(top, peak)
        total = None
        for s in range(slots):
            e = jnp.exp2((probs[s] - top) * rate + biases[s])
            probs[s] = e
            part = jnp.sum(e, axis=0, keepdims=True)
            total = part if total is None else total + part
        inverse = 1.0 / total
        out_t = None
        for s in range(slots):
            p = probs[s] * inverse
            probs[s] = p
            low = p.astype(BF16)
            part = dot(kv[h, s, 1], low, 0, 0)
            out_t = part if out_t is None else out_t + part
            term = dot(low, do, 1, 0)
            if s:
                tsend[s - 1, h, 1] = term.astype(BF16)
            else:
                acc[h, 1] = term
        delta = jnp.sum(do.astype(F32).T * out_t, axis=0, keepdims=True)
        att[:, cols] = out_t.T.astype(BF16)
        gq_t = None
        for s in range(slots):
            gp = dot(kv[h, s, 1], do, 1, 1)
            gs = (probs[s] * (gp - delta)).astype(BF16)
            term = dot(gs, q, 1, 0) * scale
            if s:
                tsend[s - 1, h, 0] = term.astype(BF16)
            else:
                acc[h, 0] = term
            part = dot(kv[h, s, 0], gs, 0, 0)
            gq_t = part if gq_t is None else gq_t + part
        gq[:, cols] = (gq_t * scale).T.astype(BF16)
        def send_swap_term(side):
            if swap is None:
                return
            ok = jnp.logical_and(side, jnp.logical_not(late))
            if relays:
                ok = jnp.logical_and(ok, jnp.logical_not(relaying))
            pl.when(ok)(lambda: term_copy(swap, h).start())
            now = jnp.logical_and(jnp.logical_and(side, holding), h >= hold)
            pl.when(now)(lambda: term_copy(swap, h - hold).start())

        send_swap_term(c != 0)
        for s in reversed(range(1, slots)):
            if s != swap:
                when(source[s][1], lambda s=s: term_copy(s, h).start())
        send_swap_term(c == 0)
        for r in relays:
            now = jnp.logical_and(hands_on[r], h >= lag)
            when(now, lambda r=r: hand_back(r, h - lag))
        return carry

    lax.fori_loop(0, heads, head, 0)

    def send_rest():
        def body(h, carry):
            term_copy(swap, h).start()
            return carry

        lax.fori_loop(heads - hold, heads, body, 0)

    if swap is not None:
        when(holding, send_rest)

    def hand_back_rest(r):
        def body(h, carry):
            hand_back(r, h)
            return carry

        lax.fori_loop(heads - lag, heads, body, 0)

    for r in relays:
        when(hands_on[r], lambda r=r: hand_back_rest(r))

    wide = 256 if half % 256 == 0 else HD

    def project_other(j, carry):
        at = pl.multiple_of(j * wide, wide)
        msend[:, pl.ds(at, wide)] = dot(
            att[...], wb[pl.ds(pl.multiple_of(theirs + at, wide), wide), :], 1, 1
        ).astype(BF16)
        return carry

    lax.fori_loop(0, half // wide, project_other, 0)
    mixed_copy = partner_copy(msend, mrecv, 1)
    mixed_copy.start()

    def project_own(j, carry):
        at = pl.multiple_of(j * wide, wide)
        part = dot(att[...], wb[pl.ds(pl.multiple_of(mine + at, wide), wide), :], 1, 1)

        @pl.when(j == 0)
        def _():
            mixed_copy.wait_recv()

        mixed[:, pl.ds(at, wide)] = (part + mrecv[:, pl.ds(at, wide)].astype(F32)).astype(BF16)
        return carry

    lax.fori_loop(0, half // wide, project_own, 0)

    def finish(h, carry):
        cols = pl.ds(pl.multiple_of(h * HD, HD), HD)
        for s in reversed(range(1, slots)):

            def add(s=s):
                term_copy(s, h).wait_recv()
                acc[h] = acc[h] + trecv[s - 1, h].astype(F32)

            when(direct[s], add)
        gk[:, cols] = acc[h, 0].astype(BF16)
        gv[:, cols] = acc[h, 1].astype(BF16)
        return carry

    lax.fori_loop(0, heads, finish, 0)

    mixed_copy.wait_send()

    def drain(h, carry):
        for s in range(1, slots):
            when(target[s][1], lambda s=s: kv_copy(s, h).wait_send())
            when(source[s][1], lambda s=s: term_copy(s, h).wait_send())
        return carry

    lax.fori_loop(0, heads, drain, 0)


def write_out(*refs):
    sems = refs[-1]
    copies = [
        pltpu.make_async_copy(src, dst, sems.at[i])
        for i, (src, dst) in enumerate(zip(refs[:4], refs[4:8]))
    ]
    for copy in copies:
        copy.start()
    for copy in copies:
        copy.wait()


def on_device(query_tok, key_tok, value_tok, out_weight, grad_out, tile_pairs):
    rows, width = query_tok.shape
    heads = width // HD
    half = grad_out.shape[1]
    tile_count = lax.axis_size("seq")
    groups = slot_groups(tile_count)
    slots = len(groups)
    anywhere = pl.BlockSpec(memory_space=pl.ANY)
    in_vmem = pl.BlockSpec(memory_space=pltpu.VMEM)
    dma = pltpu.SemaphoreType.DMA
    near = (slots - 1, heads)
    held = pl.pallas_call(
        functools.partial(kernel, groups, tile_count, HD ** (-0.5)),
        out_shape=(
            pltpu.VMEM((rows, half), BF16),
            pltpu.VMEM((rows, width), BF16),
            pltpu.VMEM((rows, width), BF16),
            pltpu.VMEM((rows, width), BF16),
        ),
        in_specs=[anywhere] * 6,
        out_specs=(in_vmem,) * 4,
        scratch_shapes=[
            pltpu.SMEM(tile_pairs.shape, jnp.int32),
            pltpu.VMEM((heads, slots, 2, rows, HD), BF16),
            pltpu.VMEM((heads, rows, HD), BF16),
            pltpu.VMEM(out_weight.shape, BF16),
            pltpu.VMEM((rows, half), BF16),
            pltpu.VMEM((rows, half), BF16),
            pltpu.VMEM((heads, rows, HD), F32),
            pltpu.VMEM((heads, rows, HD), BF16),
            pltpu.VMEM((rows, width), BF16),
            pltpu.VMEM((slots, rows, rows), F32),
            pltpu.VMEM((heads, 2, rows, HD), F32),
            pltpu.VMEM(near + (2, rows, HD), BF16),
            pltpu.VMEM(near + (2, rows, HD), BF16),
            pltpu.VMEM((rows, half), BF16),
            pltpu.VMEM((rows, half), BF16),
            pltpu.SemaphoreType.REGULAR,
            dma((3 * heads + 3,)),
            dma(near),
            dma(near),
            dma(near),
            dma(near),
            dma((2,)),
            dma((2,)),
        ],
        compiler_params=pltpu.CompilerParams(
            collective_id=0, has_side_effects=True, vmem_limit_bytes=52 * 2**20
        ),
        name="tile_attention",
    )(pltpu.with_memory_space_constraint(tile_pairs, pltpu.HBM), query_tok, key_tok, value_tok, out_weight, grad_out)
    return pl.pallas_call(
        write_out,
        out_shape=tuple(jax.ShapeDtypeStruct(x.shape, x.dtype) for x in held),
        in_specs=[in_vmem] * 4,
        out_specs=(anywhere,) * 4,
        scratch_shapes=[dma((4,))],
        name="write_out",
    )(*[pltpu.with_memory_space_constraint(x, pltpu.VMEM) for x in held])


def solution(mesh):
    in_specs = (
        P("seq", "head"),
        P("seq", "head"),
        P("seq", "head"),
        P(None, "head"),
        P("seq", "head"),
        P("seq", None),
    )
    out_specs = (P("seq", "head"), P("seq", "head"), P("seq", "head"), P("seq", "head"))
    return jax.shard_map(
        on_device, mesh=mesh, in_specs=in_specs, out_specs=out_specs, check_vma=False
    )
```

```python
import functools

import jax
import jax.numpy as jnp
from jax import lax
from jax.experimental import pallas as pl
from jax.experimental.pallas import tpu as pltpu
from jax.sharding import PartitionSpec as P

HD = 128
GW_T = 8
MASKED = -1e30
LOG2E = 1.4426950408889634
MESH = pl.DeviceIdType.MESH
F32 = jnp.float32
BF16 = jnp.bfloat16


def slot_groups(tile_count):
    frame_tiles = min(4, tile_count // 8) * GW_T
    offsets = (0, 1, -1, GW_T, -GW_T, frame_tiles, -frame_tiles)
    groups = []
    for column, offset in enumerate(offsets):
        if abs(offset) >= tile_count:
            continue
        for group in groups:
            if (group[0] - offset) % tile_count == 0:
                group[1] = True
                group[2].append(column)
                break
        else:
            groups.append([offset, False, [column]])
    return groups


def dot(a, b, da, db):
    return lax.dot_general(a, b, (((da,), (db,)), ((), ())), preferred_element_type=F32)


def kernel(
    groups, tile_count, scale,
    pairs_in, q_in, k_in, v_in, w_in, g_in,
    mixed, gq, gk, gv,
    pairs, kv, qb, wb, gown, goth, gacc, dob, att, probs, acc, tsend, trecv, msend, mrecv,
    ready, load_sem, kv_send, kv_recv, t_send, t_recv, x_send, x_recv,
):
    g = lax.axis_index("seq")
    c = lax.axis_index("head")
    other = 1 - c
    heads = qb.shape[0]
    rows = qb.shape[1]
    half = gown.shape[1]
    slots = len(groups)

    def place(step, wraps):
        at = g + step
        if wraps:
            return lax.rem(at + tile_count, tile_count), None
        ok = jnp.logical_and(at >= 0, at < tile_count)
        return jnp.clip(at, 0, tile_count - 1), ok

    def when(ok, fn):
        if ok is None:
            fn()
        else:
            pl.when(ok)(fn)

    source = [place(o, w) for o, w, _ in groups]
    target = [place(-o, w) for o, w, _ in groups]
    swaps = [s for s, (_, w, _) in enumerate(groups) if w]
    swap = swaps[0] if swaps else None
    hands_on = [None] * slots
    middle = tile_count // 2
    if swap is not None:
        for s, (o, _, _) in enumerate(groups):
            if abs(o) != 1:
                continue
            ends, near = ((tile_count - 1, middle), (0, middle - 1))[o > 0]
            relay = g == ends
            hands_on[s] = relay
            to, ok = target[s]
            crossing = g == (2 * middle - 1) - near
            target[s] = (
                jnp.where(relay, near, to),
                jnp.logical_or(relay, jnp.logical_and(ok, jnp.logical_not(crossing))),
            )
            at, ok = source[s]
            source[s] = (jnp.where(g == near, ends, at), ok)
    direct = [
        ok if hand is None else jnp.logical_and(ok, jnp.logical_not(hand))
        for (_, ok), hand in zip(target, hands_on)
    ]
    relays = [s for s in range(slots) if hands_on[s] is not None]
    relaying = None
    for s in relays:
        relaying = hands_on[s] if relaying is None else jnp.logical_or(relaying, hands_on[s])
    order = [0] + ([swap] if swap is not None else [])
    order += [s for s in range(slots) if s not in order]
    ahead = min(2, heads)

    barrier = pltpu.get_barrier_semaphore()
    pl.semaphore_signal(barrier, inc=1, device_id=(g, other), device_id_type=MESH)
    peers = 1
    answers = [(0, middle - 1), (middle, tile_count - 1)]
    if middle >= 4:
        answers.append((middle + middle // 2, middle + middle // 2 - 1))
    if not relays:
        answers = []
    for to, ok in target[1:] + [source[s] for s in range(1, slots) if s != swap]:
        greets, counts = ok, ok
        for early, late in answers:
            greets = jnp.logical_and(greets, jnp.logical_not((g == late) & (to == early))) if ok is not None else None
            counts = jnp.logical_and(counts, jnp.logical_not((g == early) & (to == late))) if ok is not None else None

        def greet(to=to):
            pl.semaphore_signal(barrier, inc=1, device_id=(to, c), device_id_type=MESH)

        when(greets, greet)
        peers = peers + (1 if counts is None else counts.astype(jnp.int32))

    loads = []

    def load(src, dst):
        copy = pltpu.make_async_copy(src, dst, load_sem.at[len(loads)])
        copy.start()
        loads.append(copy)
        return copy

    kv_loads = []
    for h in range(heads):
        cols = pl.ds(h * HD, HD)
        kv_loads.append(
            (load(k_in.at[:, cols], kv.at[h, 0, 0]), load(v_in.at[:, cols], kv.at[h, 0, 1]))
        )
    own_load = load(g_in, gown)
    pairs_load = load(pairs_in, pairs)
    w_load = load(w_in, wb)
    q_loads = [load(q_in.at[:, pl.ds(h * HD, HD)], qb.at[h]) for h in range(heads)]

    pl.semaphore_wait(barrier, peers)
    for early, late in answers:

        def answer(early=early):
            pl.semaphore_signal(ready, inc=1, device_id=(early, c), device_id_type=MESH)

        pl.when(g == late)(answer)

    def hear():
        pl.semaphore_wait(ready, 1)

    def partner_copy(src, dst, i):
        return pltpu.make_async_remote_copy(
            src_ref=src, dst_ref=dst, send_sem=x_send.at[i], recv_sem=x_recv.at[i],
            device_id=(g, other), device_id_type=MESH,
        )

    def kv_copy(s, h, held=0):
        return pltpu.make_async_remote_copy(
            src_ref=kv.at[h, held], dst_ref=kv.at[h, s],
            send_sem=kv_send.at[s - 1, h], recv_sem=kv_recv.at[s - 1, h],
            device_id=(target[s][0], c), device_id_type=MESH,
        )

    def term_copy(s, h):
        return pltpu.make_async_remote_copy(
            src_ref=tsend.at[s - 1, h], dst_ref=trecv.at[s - 1, h],
            send_sem=t_send.at[s - 1, h], recv_sem=t_recv.at[s - 1, h],
            device_id=(source[s][0], c), device_id_type=MESH,
        )

    def send_swap_tile(h, side=None):
        if swap is None or h >= heads:
            return
        ok = side
        if h >= ahead and relays:
            ok = jnp.logical_not(relaying)
            ok = ok if side is None else jnp.logical_and(side, ok)
        when(ok, lambda: kv_copy(swap, h).start())

    for copy in kv_loads[0]:
        copy.wait()
    send_swap_tile(0)
    if len(answers) > 2:
        pl.when(g == answers[2][0])(hear)
    for h in range(heads):
        if h + 1 < heads:
            for copy in kv_loads[h + 1]:
                copy.wait()
        send_swap_tile(h + 1, c == 0)
        for s in reversed(range(1, slots)):
            if s != swap:
                when(direct[s], lambda s=s, h=h: kv_copy(s, h).start())
        send_swap_tile(h + 1, c != 0)
    own_load.wait()
    grad_copy = partner_copy(gown, goth, 0)
    grad_copy.start()

    for s in range(1, slots):
        if source[s][1] is not None:

            def clear(s=s):
                def body(h, carry):
                    kv[h, s] = jnp.zeros(kv.shape[2:], BF16)
                    return carry

                lax.fori_loop(0, heads, body, 0)

            pl.when(jnp.logical_not(source[s][1]))(clear)

    w_load.wait()
    mine = pl.multiple_of(c * half, half)
    theirs = pl.multiple_of(other * half, half)

    def grad_own(h, carry):
        cols = pl.ds(pl.multiple_of(h * HD, HD), HD)
        gacc[h] = dot(gown[...], wb[pl.ds(mine, half), cols], 1, 0)
        return carry

    lax.fori_loop(0, heads, grad_own, 0)
    grad_copy.wait()

    def grad_other(h, carry):
        cols = pl.ds(pl.multiple_of(h * HD, HD), HD)
        dob[h] = (gacc[h] + dot(goth[...], wb[pl.ds(theirs, half), cols], 1, 0)).astype(BF16)
        return carry

    lax.fori_loop(0, heads, grad_other, 0)
    if answers:
        pl.when(jnp.logical_or(g == answers[0][0], g == answers[1][0]))(hear)
    for copy in q_loads:
        copy.wait()

    pairs_load.wait()
    biases = []
    for _, _, columns in groups:
        there = pairs[0, columns[0]]
        for column in columns[1:]:
            there = jnp.maximum(there, pairs[0, column])
        biases.append(jnp.where(there >= 0, 0.0, MASKED).astype(F32))
    rate = scale * LOG2E
    lag = min(3, heads)
    hold = min(1, heads)
    late = 2 * lax.rem(g, middle) >= middle
    late = jnp.logical_and(late, jnp.logical_or(g != middle + middle // 2, c == 0))
    holding = jnp.logical_and(late, jnp.logical_not(relaying)) if relays else late

    def hand_back(r, h):
        term_copy(r, h).wait_recv()
        both = tsend[swap - 1, h].astype(F32) + trecv[r - 1, h].astype(F32)
        tsend[swap - 1, h] = both.astype(BF16)
        term_copy(swap, h).start()

    def head(h, carry):
        cols = pl.ds(pl.multiple_of(h * HD, HD), HD)
        q = qb[h]
        do = dob[h]
        top = None
        for s in order:
            if s:
                when(source[s][1], lambda s=s: kv_copy(s, h).wait_recv())
            if s and s == swap:
                for r in relays:
                    when(hands_on[r], lambda r=r: kv_copy(r, h, swap).start())
                if relays:
                    now = jnp.logical_and(relaying, h + ahead < heads)
                    when(now, lambda: kv_copy(swap, h + ahead).start())
            scores = dot(kv[h, s, 0], q, 1, 1)
            probs[s] = scores
            peak = jnp.max(scores, axis=0, keepdims=True) + biases[s]
            top = peak if top is None else jnp.maximum(top, peak)
        total = None
        for s in range(slots):
            e = jnp.exp2((probs[s] - top) * rate + biases[s])
            probs[s] = e
            part = jnp.sum(e, axis=0, keepdims=True)
            total = part if total is None else total + part
        inverse = 1.0 / total
        out_t = None
        for s in range(slots):
            p = probs[s] * inverse
            probs[s] = p
            low = p.astype(BF16)
            part = dot(kv[h, s, 1], low, 0, 0)
            out_t = part if out_t is None else out_t + part
            term = dot(low, do, 1, 0)
            if s:
                tsend[s - 1, h, 1] = term.astype(BF16)
            else:
                acc[h, 1] = term
        delta = jnp.sum(do.astype(F32).T * out_t, axis=0, keepdims=True)
        att[:, cols] = out_t.T.astype(BF16)
        gq_t = None
        for s in range(slots):
            gp = dot(kv[h, s, 1], do, 1, 1)
            gs = (probs[s] * (gp - delta)).astype(BF16)
            term = dot(gs, q, 1, 0) * scale
            if s:
                tsend[s - 1, h, 0] = term.astype(BF16)
            else:
                acc[h, 0] = term
            part = dot(kv[h, s, 0], gs, 0, 0)
            gq_t = part if gq_t is None else gq_t + part
        gq[:, cols] = (gq_t * scale).T.astype(BF16)
        def send_swap_term(side):
            if swap is None:
                return
            ok = jnp.logical_and(side, jnp.logical_not(late))
            if relays:
                ok = jnp.logical_and(ok, jnp.logical_not(relaying))
            pl.when(ok)(lambda: term_copy(swap, h).start())
            now = jnp.logical_and(jnp.logical_and(side, holding), h >= hold)
            pl.when(now)(lambda: term_copy(swap, h - hold).start())

        send_swap_term(c != 0)
        for s in reversed(range(1, slots)):
            if s != swap:
                when(source[s][1], lambda s=s: term_copy(s, h).start())
        send_swap_term(c == 0)
        for r in relays:
            now = jnp.logical_and(hands_on[r], h >= lag)
            when(now, lambda r=r: hand_back(r, h - lag))
        return carry

    lax.fori_loop(0, heads, head, 0)

    def send_rest():
        def body(h, carry):
            term_copy(swap, h).start()
            return carry

        lax.fori_loop(heads - hold, heads, body, 0)

    if swap is not None:
        when(holding, send_rest)

    def hand_back_rest(r):
        def body(h, carry):
            hand_back(r, h)
            return carry

        lax.fori_loop(heads - lag, heads, body, 0)

    for r in relays:
        when(hands_on[r], lambda r=r: hand_back_rest(r))

    wide = 256 if half % 256 == 0 else HD

    def project_other(j, carry):
        at = pl.multiple_of(j * wide, wide)
        msend[:, pl.ds(at, wide)] = dot(
            att[...], wb[pl.ds(pl.multiple_of(theirs + at, wide), wide), :], 1, 1
        ).astype(BF16)
        return carry

    lax.fori_loop(0, half // wide, project_other, 0)
    mixed_copy = partner_copy(msend, mrecv, 1)
    mixed_copy.start()

    def project_own(j, carry):
        at = pl.multiple_of(j * wide, wide)
        part = dot(att[...], wb[pl.ds(pl.multiple_of(mine + at, wide), wide), :], 1, 1)

        @pl.when(j == 0)
        def _():
            mixed_copy.wait_recv()

        mixed[:, pl.ds(at, wide)] = (part + mrecv[:, pl.ds(at, wide)].astype(F32)).astype(BF16)
        return carry

    lax.fori_loop(0, half // wide, project_own, 0)

    def finish(h, carry):
        cols = pl.ds(pl.multiple_of(h * HD, HD), HD)
        for s in reversed(range(1, slots)):

            def add(s=s):
                term_copy(s, h).wait_recv()
                acc[h] = acc[h] + trecv[s - 1, h].astype(F32)

            when(direct[s], add)
        gk[:, cols] = acc[h, 0].astype(BF16)
        gv[:, cols] = acc[h, 1].astype(BF16)
        return carry

    lax.fori_loop(0, heads, finish, 0)

    mixed_copy.wait_send()

    def drain(h, carry):
        for s in range(1, slots):
            when(target[s][1], lambda s=s: kv_copy(s, h).wait_send())
            when(source[s][1], lambda s=s: term_copy(s, h).wait_send())
        return carry

    lax.fori_loop(0, heads, drain, 0)


def write_out(*refs):
    sems = refs[-1]
    copies = [
        pltpu.make_async_copy(src, dst, sems.at[i])
        for i, (src, dst) in enumerate(zip(refs[:4], refs[4:8]))
    ]
    for copy in copies:
        copy.start()
    for copy in copies:
        copy.wait()


def on_device(query_tok, key_tok, value_tok, out_weight, grad_out, tile_pairs):
    rows, width = query_tok.shape
    heads = width // HD
    half = grad_out.shape[1]
    tile_count = lax.axis_size("seq")
    groups = slot_groups(tile_count)
    slots = len(groups)
    anywhere = pl.BlockSpec(memory_space=pl.ANY)
    in_vmem = pl.BlockSpec(memory_space=pltpu.VMEM)
    dma = pltpu.SemaphoreType.DMA
    near = (slots - 1, heads)
    held = pl.pallas_call(
        functools.partial(kernel, groups, tile_count, HD ** (-0.5)),
        out_shape=(
            pltpu.VMEM((rows, half), BF16),
            pltpu.VMEM((rows, width), BF16),
            pltpu.VMEM((rows, width), BF16),
            pltpu.VMEM((rows, width), BF16),
        ),
        in_specs=[anywhere] * 6,
        out_specs=(in_vmem,) * 4,
        scratch_shapes=[
            pltpu.SMEM(tile_pairs.shape, jnp.int32),
            pltpu.VMEM((heads, slots, 2, rows, HD), BF16),
            pltpu.VMEM((heads, rows, HD), BF16),
            pltpu.VMEM(out_weight.shape, BF16),
            pltpu.VMEM((rows, half), BF16),
            pltpu.VMEM((rows, half), BF16),
            pltpu.VMEM((heads, rows, HD), F32),
            pltpu.VMEM((heads, rows, HD), BF16),
            pltpu.VMEM((rows, width), BF16),
            pltpu.VMEM((slots, rows, rows), F32),
            pltpu.VMEM((heads, 2, rows, HD), F32),
            pltpu.VMEM(near + (2, rows, HD), BF16),
            pltpu.VMEM(near + (2, rows, HD), BF16),
            pltpu.VMEM((rows, half), BF16),
            pltpu.VMEM((rows, half), BF16),
            pltpu.SemaphoreType.REGULAR,
            dma((3 * heads + 3,)),
            dma(near),
            dma(near),
            dma(near),
            dma(near),
            dma((2,)),
            dma((2,)),
        ],
        compiler_params=pltpu.CompilerParams(
            collective_id=0, has_side_effects=True, vmem_limit_bytes=52 * 2**20
        ),
        name="tile_attention",
    )(pltpu.with_memory_space_constraint(tile_pairs, pltpu.HBM), query_tok, key_tok, value_tok, out_weight, grad_out)
    return pl.pallas_call(
        write_out,
        out_shape=tuple(jax.ShapeDtypeStruct(x.shape, x.dtype) for x in held),
        in_specs=[in_vmem] * 4,
        out_specs=(anywhere,) * 4,
        scratch_shapes=[dma((4,))],
        name="write_out",
    )(*[pltpu.with_memory_space_constraint(x, pltpu.VMEM) for x in held])


def solution(mesh):
    in_specs = (
        P("seq", "head"),
        P("seq", "head"),
        P("seq", "head"),
        P(None, "head"),
        P("seq", "head"),
        P("seq", None),
    )
    out_specs = (P("seq", "head"), P("seq", "head"), P("seq", "head"), P("seq", "head"))
    return jax.shard_map(
        on_device, mesh=mesh, in_specs=in_specs, out_specs=out_specs, check_vma=False
    )
```
